256 devices in a mesh: sec: 2 (over y_hi), col: 8 (over z), row: 16 (over y_lo, x, core).
Axes of the slice: x: 4, y: 4 (y_hi: 2, y_lo: 2; y = y_hi * 2 + y_lo), z: 8, core: 2. Of those that a mesh axis runs over, the one named last changes fastest.
Arguments:
- ancestor: float32 [16384, 16384], P('row', ('sec', 'col')), may hold values from -0.3 to 0.3
- panel: float32 [2, 8192, 2048], P('sec', 'row', 'col'), may hold values from -1.5 to 1.5
- diag_inverse: float32 [2, 2048, 2048], P('sec', 'col', 'row'), may hold values from -12 to 12
- frontier: int32 [2, 16, 4], replicated, may hold values from 0 to 7, as said below
- counts: int32 [2, 16], replicated, may hold values from 1 to 4
- pattern: int32 [2, 64, 64], replicated, may hold values 0 or 1
Outputs:
- cross_block: float32 [2, 2048, 8192], P('sec', 'col', 'row')
- inverse: float32 [2, 2048, 2048], P('sec', 'col', 'row')
The draws below stay inside these ranges and needn't reach their ends.
Inputs may be any that keep to these rules, and one draw needn't show every extreme that they name: The 4 offsets of one child and group are distinct; slot j of group g is ancestor tile 8 * g + frontier[c, g, j]. Slots j >= counts[c, g] of group g are padding for child c.
All inputs are finite; a program needn't handle non-finite values.
Results may differ from the reference program's by a relative error of at most 0.0001.
Values sent between devices are 32-bit elements; how exact they have to be, the bound alone decides.
No kernel may reach another device: no remote copies, remote signals or barrier semaphores. Data moves between devices by JAX's collectives and lax.ppermute only.
A program may use at most 128 MiB of HBM per device.

```python
import jax
import jax.numpy as jnp
from jax import lax

ORDER = 16384
PANEL = 2048
TILE = 128
GROUP = 8
SLOTS = 4
GROUPS = 16
FSLOTS = 64
FRONT = 8192


def draw_frontier(key, part):
    scores = jax.random.randint(key, (2, GROUPS, GROUP), 0, 1 << 20)
    scores = scores * GROUP + jnp.arange(GROUP, dtype=jnp.int32)
    ordering = jnp.argsort(scores, axis=-1, stable=True)
    return ordering[:, :, :SLOTS].astype(jnp.int32)


def place_ends(array, rng, low, top_value):
    longest = array.shape.index(max(array.shape))
    spots = []
    for shift in (0, 1):
        where = [jax.random.randint(jax.random.fold_in(rng, axis), (), 0, length) for axis, length in enumerate(array.shape)]
        where[longest] = (where[longest] + shift) % array.shape[longest]
        spots.append(tuple(where))
    return array.at[spots[0]].set(low).at[spots[1]].set(top_value)


def level_of(key, shape, cuts, smallest, largest):
    def one(axis_at, parts):
        heights = jax.random.uniform(jax.random.fold_in(jax.random.fold_in(key, 6), axis_at), (parts,), jnp.float32, smallest / len(cuts), largest / len(cuts))
        return jnp.repeat(jnp.exp(heights), shape[axis_at] // parts).reshape((-1,) + (1,) * (len(shape) - axis_at - 1))

    gain = one(*cuts[0])
    for cut in cuts[1:]:
        gain = gain * one(*cut)
    return gain


def centred(stream_key, dims, scale, limit, split=(), kind=jnp.bfloat16):
    drawn = scale * jax.random.normal(stream_key, dims, jnp.float32)
    if split:
        drawn = drawn * level_of(stream_key, dims, split, -0.22, 0.18)
    return jnp.clip(drawn, -limit, limit).astype(kind)


def setup_inputs(seed: int = 0) -> dict:
    seeds = jax.random.split(jax.random.key(seed), 7)
    return {
        "ancestor": centred(seeds[0], (ORDER, ORDER), 0.05, 0.3, ((0, 16), (1, 16)), jnp.float32),
        "panel": centred(seeds[1], (2, FRONT, PANEL), 0.25, 1.5, ((0, 2), (1, 16), (2, 8)), jnp.float32),
        "diag_inverse": centred(seeds[2], (2, PANEL, PANEL), 2.0, 12.0, ((0, 2), (1, 8), (2, 16)), jnp.float32),
        "frontier": draw_frontier(jax.random.fold_in(seeds[6], 71), 0),
        "counts": place_ends(jax.random.randint(seeds[4], (2, GROUPS), 1, SLOTS + 1), jax.random.fold_in(seeds[4], 1), 1, SLOTS).astype(jnp.int32),
        "pattern": place_ends((jax.random.randint(seeds[5], (2, FSLOTS, FSLOTS), 0, 5) < 3).astype(jnp.int32), jax.random.fold_in(seeds[5], 1), 0, 1),
    }


def reference(ancestor, panel, diag_inverse, frontier, counts, pattern):
    cross_list = []
    inverse_list = []
    for child_id in range(2):
        slot_ids = jnp.arange(SLOTS).astype(jnp.int32)
        group_ids = jnp.arange(GROUPS).astype(jnp.int32)
        tile_ids = (group_ids[:, None] * GROUP + frontier[child_id].astype(jnp.int32)).reshape(-1)
        alive_slots = (slot_ids[None, :] < counts[child_id][:, None]).reshape(-1).astype(jnp.float32)
        within = jnp.arange(TILE).astype(jnp.int32)
        indices = (tile_ids[:, None] * TILE + within[None, :]).reshape(-1)
        picked = jnp.take(jnp.take(ancestor, indices, axis=0), indices, axis=1)
        tile_mask = pattern[child_id].astype(jnp.float32) * alive_slots[:, None] * alive_slots[None, :]
        picked = (picked.reshape(FSLOTS, TILE, FSLOTS, TILE) * tile_mask[:, None, :, None]).reshape(FRONT, FRONT)
        product = jnp.dot(picked, panel[child_id], precision=lax.Precision.HIGHEST, preferred_element_type=jnp.float32)
        cross_part = -product.T
        inverse_part = diag_inverse[child_id] - jnp.dot(cross_part, panel[child_id], precision=lax.Precision.HIGHEST, preferred_element_type=jnp.float32)
        cross_list.append(cross_part)
        inverse_list.append(inverse_part)
    return jnp.stack(cross_list), jnp.stack(inverse_list)
```

```python
import jax
import jax.numpy as jnp
from jax import lax
from jax.experimental import pallas as pl
from jax.experimental.pallas import tpu as pltpu
from jax.sharding import PartitionSpec as P

TILE = 128
GROUP = 8
SLOTS = 4


Z, Y, X, CORES = 8, 2, 4, 2


def row_of(y, x, c):
    return (y % Y) * X * CORES + (x % X) * CORES + c


def row_pairs(move):
    places = [(y, x, c) for y in range(Y) for x in range(X) for c in range(CORES)]
    return [(row_of(*place), row_of(*move(*place))) for place in places]


def along_x(value, step):
    return lax.ppermute(value, "row", row_pairs(lambda y, x, c: (y, x + step, c)))


def across_y(value):
    return lax.ppermute(value, "row", row_pairs(lambda y, x, c: (y + 1, x, c)))


def across_core(value):
    return lax.ppermute(value, "row", row_pairs(lambda y, x, c: (y, x, 1 - c)))


def across_sec(value):
    return lax.ppermute(value, "sec", [(0, 1), (1, 0)])


def along_z(value, step):
    return lax.ppermute(value, "col", [(z, (z + step) % Z) for z in range(Z)])


def dot(left, right, dims):
    return lax.dot_general(
        left,
        right,
        (dims, ((), ())),
        precision=lax.Precision.HIGH,
        preferred_element_type=jnp.float32,
    )


def pick_kernel(place, frontier, counts, pattern, rows_ref, out_ref):
    sec, own_block, group = place[0], place[1], place[2]
    slot = pl.program_id(1)
    child = lax.rem(sec + pl.program_id(0), 2)
    row_live = slot < counts[child, group]
    for other in range(SLOTS):
        keep = row_live & (other < counts[child, own_block])
        mask = jnp.where(keep, pattern[child, group * SLOTS + slot, own_block * SLOTS + other], 0)
        start = pl.multiple_of(frontier[child, own_block, other] * TILE, TILE)
        tile = rows_ref[:, pl.ds(start, TILE)]
        out_ref[:, other * TILE : (other + 1) * TILE] = tile * mask.astype(jnp.float32)


def pick_tiles(ancestor, frontier, counts, pattern, sec, own_block, group):
    def rows_map(which, slot, place, frontier, counts, pattern):
        return (frontier[lax.rem(place[0] + which, 2), place[2], slot], 0)

    place = jnp.stack([sec, own_block, group]).astype(jnp.int32)
    edge = SLOTS * TILE
    return pl.pallas_call(
        pick_kernel,
        grid_spec=pltpu.PrefetchScalarGridSpec(
            num_scalar_prefetch=4,
            grid=(2, SLOTS),
            in_specs=[pl.BlockSpec((TILE, GROUP * TILE), rows_map)],
            out_specs=pl.BlockSpec((None, TILE, edge), lambda which, slot, *_: (which, slot, 0)),
        ),
        out_shape=jax.ShapeDtypeStruct((2, edge, edge), jnp.float32),
        name="pick_tiles",
    )(place, frontier, counts, pattern, ancestor)


def to_columns(panel):
    low, high = panel[:, :TILE], panel[:, TILE:]
    y = lax.axis_index("row") // (X * CORES)
    first = jnp.where(y == 0, low, high)
    second = jnp.where(y == 0, high, low)

    def in_plane(flip):
        pairs = []
        for z in range(Z):
            for g in range(16):
                c = (g // Z) ^ flip
                chip = (z + g % Z + 4 * c) % Z
                pairs.append((z * 16 + g, z * 16 + chip * CORES + c))
        return pairs

    first = lax.ppermute(first, ("col", "row"), in_plane(0))
    second = lax.ppermute(second, ("col", "row"), in_plane(1))
    both = jnp.concatenate([first, second], axis=0)
    mirror = []
    for z in range(Z):
        for chip in range(8):
            for c in range(CORES):
                mirror.append(
                    (z * 16 + chip * CORES + c, (chip - z + 4 * c) % Z * 16 + chip * CORES + c)
                )
    return lax.ppermute(both, ("col", "row"), mirror)


def gathered_in_plane(own):
    left, right, over = along_x(own, 1), along_x(own, -1), across_y(own)
    far = along_x(left, 1)
    over_right = along_x(over, -1)
    over_left = across_y(left)
    one, two = 344, 688
    over_far = jnp.concatenate(
        [
            along_x(over_left[:one], 1),
            along_x(over_right[one:two], -1),
            across_y(far[two:]),
        ],
        axis=0,
    )
    return [
        (0, 0, own),
        (0, 3, left),
        (0, 1, right),
        (1, 0, over),
        (0, 2, far),
        (1, 1, over_right),
        (1, 3, over_left),
        (1, 2, over_far),
    ]


def gathered_along_z(own):
    half = own.shape[0] // 2
    up, down = [own], [own]
    for _ in range(3):
        up.append(along_z(up[-1], 1))
        down.append(along_z(down[-1], -1))
    far = jnp.concatenate([along_z(up[3][:half], 1), along_z(down[3][half:], -1)], axis=0)
    return jnp.stack([own, down[1], down[2], down[3], far, up[3], up[2], up[1]])


def scattered_along_z(parts):
    half = parts.shape[1] // 2

    def term(distance, which):
        return parts[distance % Z, which * half : (which + 1) * half]

    up_a, down_b = along_z(term(4, 0), 1), along_z(term(4, 1), -1)
    up_b, down_a = along_z(term(3, 1), 1), along_z(term(-3, 0), -1)
    up_a, down_b = along_z(up_a + term(3, 0), 1), along_z(down_b + term(-3, 1), -1)
    for distance in (2, 1):
        up_b = along_z(up_b + term(distance, 1), 1)
        down_a = along_z(down_a + term(-distance, 0), -1)
        up_a = along_z(up_a + term(distance, 0), 1)
        down_b = along_z(down_b + term(-distance, 1), -1)
    return jnp.concatenate([term(0, 0) + up_a + down_a, term(0, 1) + up_b + down_b], axis=0)


def scattered_in_plane(term):
    far = term(1, 2)
    one, two = 88, 176
    from_left, from_right, from_over = (
        along_x(far[:one], 1),
        along_x(far[one:two], -1),
        across_y(far[two:]),
    )

    def added(block, piece, start):
        rows = piece.shape[0]
        return jnp.concatenate(
            [block[:start], block[start : start + rows] + piece, block[start + rows :]], axis=0
        )

    over_right = added(term(1, 1), from_left, 0)
    over_left = added(term(1, 3), from_right, one)
    row_far = added(term(0, 2), from_over, two)
    right = term(0, 1) + along_x(row_far, 1) + across_y(over_right)
    over = term(1, 0) + along_x(over_left, -1)
    return term(0, 0) + along_x(right, 1) + along_x(term(0, 3), -1) + across_y(over)


def per_device(ancestor, panel, diag_inverse, frontier, counts, pattern):
    s = lax.axis_index("sec")
    z = lax.axis_index("col")
    row = lax.axis_index("row")
    y, x, c = row // 8, row // 2 % 4, row % 2
    edge = SLOTS * TILE

    columns_own = to_columns(panel[0])

    picked = pick_tiles(ancestor, frontier, counts, pattern, s, s * Z + z, row)
    partner = across_sec(picked[1])
    mine = picked[0]
    tiles = jnp.where(
        s == c,
        jnp.concatenate([mine, partner], axis=1),
        jnp.concatenate([partner, mine], axis=1),
    )
    sibling = across_core(tiles)
    tiles = jnp.concatenate(
        [tiles, jnp.concatenate([sibling[:, edge:], sibling[:, :edge]], axis=1)], axis=0
    )

    low, high = panel[0][:, :TILE], panel[0][:, TILE:]
    sibling_rows = across_core(jnp.where(c == 0, high, low))
    rows_own = jnp.concatenate([jnp.where(c == 0, low, high), sibling_rows], axis=0)
    rows_full = gathered_along_z(rows_own)

    parts = jnp.zeros((Z, TILE, 2 * edge), jnp.float32)
    for dy, dx, block in gathered_in_plane(columns_own):
        chip = (y + dy) % Y * X + (x + dx) % X
        distance = (chip - 2 * z + 4 * c) % Z
        part = dot(block, tiles, ((0,), (1,)))
        parts = lax.dynamic_update_slice(parts, part[None], (distance, 0, 0))
    reduced = scattered_along_z(parts)

    received = across_core(reduced)
    received = jnp.concatenate([received[:, edge:], received[:, :edge]], axis=1)
    whole = jnp.where(
        c == 0,
        jnp.concatenate([reduced, received], axis=0),
        jnp.concatenate([received, reduced], axis=0),
    )
    cross_part = -whole[:, :edge]

    products = dot(rows_full, whole, ((1,), (1,)))
    products = jnp.transpose(products, (0, 2, 1))

    def term(dy, dx):
        chip = (y + dy) % Y * X + (x + dx) % X
        return lax.dynamic_index_in_dim(products, (chip - z) % Z, 0, keepdims=False)

    inverse_part = diag_inverse[0] + scattered_in_plane(term)
    return (cross_part[None], inverse_part[None])


def solution(mesh):
    return jax.shard_map(
        per_device,
        mesh=mesh,
        in_specs=(
            P("row", ("sec", "col")),
            P("sec", "row", "col"),
            P("sec", "col", "row"),
            P(),
            P(),
            P(),
        ),
        out_specs=(P("sec", "col", "row"), P("sec", "col", "row")),
        check_vma=False,
    )
```

```python
import functools

import jax
import jax.numpy as jnp
from jax import lax
from jax.experimental import pallas as pl
from jax.experimental.pallas import tpu as pltpu
from jax.sharding import PartitionSpec as P


TILE = 128
SLOTS = 4


Z, Y, X, CORES = 8, 2, 4, 2


def row_of(y, x, c):
    return (y % Y) * X * CORES + (x % X) * CORES + c


def row_pairs(move):
    places = [(y, x, c) for y in range(Y) for x in range(X) for c in range(CORES)]
    return [(row_of(*place), row_of(*move(*place))) for place in places]


def along_x(value, step):
    return lax.ppermute(value, "row", row_pairs(lambda y, x, c: (y, x + step, c)))


def across_y(value):
    return lax.ppermute(value, "row", row_pairs(lambda y, x, c: (y + 1, x, c)))


def across_core(value):
    return lax.ppermute(value, "row", row_pairs(lambda y, x, c: (y, x, 1 - c)))


def across_sec(value):
    return lax.ppermute(value, "sec", [(0, 1), (1, 0)])


def along_z(value, step):
    return lax.ppermute(value, "col", [(z, (z + step) % Z) for z in range(Z)])


def dot(left, right, dims):
    return lax.dot_general(
        left,
        right,
        (dims, ((), ())),
        precision=lax.Precision.HIGH,
        preferred_element_type=jnp.float32,
    )


def pick_kernel(place, ancestor, out, sems):
    tiles = [(a, b) for a in range(SLOTS) for b in range(SLOTS)]

    def spot(a, b):
        return (pl.ds(a * TILE, TILE), pl.ds(b * TILE, TILE))

    copies = []
    for a, b in tiles:
        first = pl.multiple_of(place[0, a] * TILE, TILE)
        second = pl.multiple_of(place[1, b] * TILE, TILE)
        source = ancestor.at[pl.ds(first, TILE), pl.ds(second, TILE)]
        copies.append(pltpu.make_async_copy(source, out.at[spot(a, b)], sems.at[a, b]))
        copies[-1].start()
    for (a, b), copy in zip(tiles, copies):
        copy.wait()
        out[spot(a, b)] = out[spot(a, b)] * place[2 + a, b].astype(jnp.float32)


def places(frontier, counts, pattern, block, group):
    ids = jnp.arange(SLOTS, dtype=jnp.int32)

    def at(table, index):
        return lax.dynamic_index_in_dim(table, index, 1, keepdims=False)

    row_live = ids[None, :] < at(counts, group)[:, None]
    column_live = ids[None, :] < at(counts, block)[:, None]
    start = (jnp.int32(0), group * SLOTS, block * SLOTS)
    near = lax.dynamic_slice(pattern, start, (2, SLOTS, SLOTS))
    mask = jnp.where(row_live[:, :, None] & column_live[:, None, :], near, 0)
    return jnp.concatenate([at(frontier, group)[:, None], at(frontier, block)[:, None], mask], axis=1)


def pick_tiles(ancestor, place):
    edge = SLOTS * TILE
    return pl.pallas_call(
        pick_kernel,
        grid_spec=pltpu.PrefetchScalarGridSpec(
            num_scalar_prefetch=1,
            grid=(),
            in_specs=[pl.BlockSpec(memory_space=pl.ANY)],
            out_specs=pl.BlockSpec(memory_space=pltpu.VMEM),
            scratch_shapes=[pltpu.SemaphoreType.DMA((SLOTS, SLOTS))],
        ),
        out_shape=jax.ShapeDtypeStruct((edge, edge), jnp.float32),
        cost_estimate=pl.CostEstimate(
            flops=edge * edge, bytes_accessed=8 * edge * edge, transcendentals=0
        ),
        name="pick_tiles",
    )(place, ancestor)


def two_terms(value):
    high = value.astype(jnp.bfloat16)
    return high, (value - high.astype(jnp.float32)).astype(jnp.bfloat16)


def split_kernel(mine, partner, sibling_mine, sibling_partner, high, low):
    edge = SLOTS * TILE
    for i, row in enumerate(((mine, partner), (sibling_mine, sibling_partner))):
        for j, ref in enumerate(row):
            spot = (pl.ds(i * edge, edge), pl.ds(j * edge, edge))
            high[spot], low[spot] = two_terms(ref[...])


def split_tiles(*tiles):
    edge = SLOTS * TILE
    shape = jax.ShapeDtypeStruct((2 * edge, 2 * edge), jnp.bfloat16)
    return pl.pallas_call(
        split_kernel,
        out_shape=(shape, shape),
        cost_estimate=pl.CostEstimate(flops=12 * edge * edge, bytes_accessed=32 * edge * edge, transcendentals=0),
        name="split_tiles",
    )(*tiles)


STEP = 512


def partial_kernel(spots, whole, where, *refs):
    count = len(spots)
    taken = count + (not whole)
    blocks, (high, low) = refs[:taken], refs[taken : taken + 2]
    parts, block_high, block_low, total, sems = refs[-5:]
    edge = SLOTS * TILE
    k = pl.program_id(0)
    y, x, z, c, flip = (where[i] for i in range(5))

    @pl.when(k == 0)
    def _():
        for j in range(count):
            for half in range(2):
                if whole or j < count - 1:
                    start = pl.multiple_of((half ^ flip) * edge, edge)
                    value = blocks[j][pl.ds(start, edge), :]
                else:
                    value = jnp.where(flip == 0, blocks[j + half][...], blocks[j + 1 - half][...])
                spot = (pl.ds(j * TILE, TILE), pl.ds(half * edge, edge))
                block_high[spot], block_low[spot] = two_terms(value.T)

    def product(left, right):
        return lax.dot_general(
            left[...], right[...], (((1,), (1,)), ((), ())), preferred_element_type=jnp.float32
        )

    total[k] = product(block_high, high) + product(block_low, high) + product(block_high, low)

    def copies(step):
        columns = pl.ds(pl.multiple_of(step * STEP, STEP), STEP)
        found = []
        for j, (dy, dx) in enumerate(spots):
            chip = lax.rem(y + dy, Y) * X + lax.rem(x + dx, X)
            distance = lax.rem(chip + 16 - 2 * z + 4 * c, Z)
            source = total.at[step, pl.ds(j * TILE, TILE), :]
            target = parts.at[distance, :, columns]
            found.append(pltpu.make_async_copy(source, target, sems.at[step, j]))
        return found

    for copy in copies(k):
        copy.start()

    @pl.when(k == pl.num_programs(0) - 1)
    def _():
        @pl.loop(0, 2 * edge // STEP)
        def _(step):
            for copy in copies(step):
                copy.wait()


def partial_products(spots, blocks, where, high, low, parts=None):
    count = len(spots)
    edge = SLOTS * TILE
    steps = 2 * edge // STEP
    vmem = pl.BlockSpec(memory_space=pltpu.VMEM)
    anywhere = pl.BlockSpec(memory_space=pl.ANY)
    tile_rows = pl.BlockSpec((STEP, 2 * edge), lambda k, where: (k, 0))
    args = [where, *blocks, high, low]
    if parts is not None:
        args.append(parts)
    rows = count * TILE
    return pl.pallas_call(
        functools.partial(partial_kernel, spots, len(blocks) == count),
        grid_spec=pltpu.PrefetchScalarGridSpec(
            num_scalar_prefetch=1,
            grid=(steps,),
            in_specs=[vmem] * len(blocks) + [tile_rows] * 2 + [anywhere] * (parts is not None),
            out_specs=anywhere,
            scratch_shapes=[
                pltpu.VMEM((rows, 2 * edge), jnp.bfloat16),
                pltpu.VMEM((rows, 2 * edge), jnp.bfloat16),
                pltpu.VMEM((steps, rows, STEP), jnp.float32),
                pltpu.SemaphoreType.DMA((steps, count)),
            ],
        ),
        out_shape=jax.ShapeDtypeStruct((Z, TILE, 2 * edge), jnp.float32),
        input_output_aliases={} if parts is None else {len(args) - 1: 0},
        cost_estimate=pl.CostEstimate(
            flops=6 * rows * 4 * edge * edge,
            bytes_accessed=4 * edge * (4 * edge + 4 * rows),
            transcendentals=0,
        ),
        name="partial_products",
    )(*args)


def to_chips(panel):
    low, high = panel[:, :TILE], panel[:, TILE:]
    y = lax.axis_index("row") // (X * CORES)
    first = jnp.where(y == 0, low, high)
    second = jnp.where(y == 0, high, low)

    def pairs(flip):
        found = []
        for z in range(Z):
            for g in range(16):
                c = (g // Z) ^ flip
                chip = (z + g % Z + 4 * c) % Z
                found.append((z * 16 + g, z * 16 + chip * CORES + c))
        return found

    first = lax.ppermute(first, ("col", "row"), pairs(0))
    second = lax.ppermute(second, ("col", "row"), pairs(1))
    return first, second


def mirrored(value):
    pairs = []
    for z in range(Z):
        for chip in range(8):
            for c in range(CORES):
                place = chip * CORES + c
                pairs.append((z * 16 + place, (chip - z + 4 * c) % Z * 16 + place))
    return lax.ppermute(value, ("col", "row"), pairs)


def scattered_along_z(parts):
    half = parts.shape[1] // 2

    def term(distance, which):
        return parts[distance % Z, which * half : (which + 1) * half]

    up_a, down_b = along_z(term(4, 0), 1), along_z(term(4, 1), -1)
    up_b, down_a = along_z(term(3, 1), 1), along_z(term(-3, 0), -1)
    for distance in (3, 2, 1):
        sums = up_a + term(distance, 0), down_b + term(-distance, 1)
        up_a, down_b = along_z(sums[0], 1), along_z(sums[1], -1)
        if distance > 1:
            up_b, down_a, *_ = together(up_b, down_a, *sums)
            sums = up_b + term(distance - 1, 1), down_a + term(1 - distance, 0)
            up_b, down_a = along_z(sums[0], 1), along_z(sums[1], -1)
            up_a, down_b, *_ = together(up_a, down_b, *sums)
    return jnp.concatenate([term(0, 0) + up_a + down_a, term(0, 1) + up_b + down_b], axis=0)


def scattered_in_plane(terms):
    groups = []
    for z in range(Z):
        for c in range(CORES):
            groups.append([z * 16 + (z + d) % Z * CORES + c for d in range(Z)])
    arrived = lax.all_to_all(terms, ("col", "row"), 0, 0, axis_index_groups=groups, tiled=True)
    return jnp.sum(arrived, axis=0)


def together(*values):
    return lax.optimization_barrier(values)


def per_device(ancestor, panel, diag_inverse, frontier, counts, pattern):
    s = lax.axis_index("sec")
    z = lax.axis_index("col")
    row = lax.axis_index("row")
    y, x, c = row // 8, row // 2 % 4, row % 2
    edge = SLOTS * TILE

    both_places = places(frontier, counts, pattern, s * Z + z, row)

    def pick(child):
        place = lax.dynamic_index_in_dim(both_places, child, 0, keepdims=False)
        return pick_tiles(ancestor, place)

    low, high = panel[0][:, :TILE], panel[0][:, TILE:]
    first, second = to_chips(panel[0])
    sibling_rows = across_core(jnp.where(c == 0, high, low))
    own_rows = jnp.concatenate([jnp.where(c == 0, low, high), sibling_rows], axis=0)
    up1 = along_z(own_rows, 1)
    down1 = along_z(own_rows, -1)
    theirs = pick(1 - s)
    partner = across_sec(theirs)
    own_columns = mirrored(jnp.concatenate([first, second], axis=0))
    mine = pick(s)
    sibling_mine = across_core(mine)
    sibling_partner = across_core(partner)
    tiles_high, tiles_low = split_tiles(mine, partner, sibling_mine, sibling_partner)

    where = jnp.stack([y, x, z, c, s ^ c]).astype(jnp.int32)

    def placed(spots, blocks, parts=None):
        return partial_products(spots, blocks, where, tiles_high, tiles_low, parts)

    left = along_x(own_columns, 1)
    right = along_x(own_columns, -1)
    over = across_y(own_columns)
    up2 = along_z(up1, 1)
    down2 = along_z(down1, -1)
    far = along_x(left, 1)
    over_right = along_x(over, -1)
    over_left = across_y(left)
    up3 = along_z(up2, 1)
    down3 = along_z(down2, -1)
    half = SLOTS * TILE
    spots = ((0, 3), (0, 1), (1, 0), (0, 0))
    parts = placed(spots, [left, right, over, own_columns])
    far_a = along_x(over_left[:half], 1)
    far_b = along_x(over_right[half:], -1)
    up4 = along_z(up3[:half], 1)
    down4 = along_z(down3[half:], -1)
    z_far = jnp.concatenate([up4, down4], axis=0)
    spots = ((0, 2), (1, 1), (1, 3), (1, 2))
    parts = placed(spots, [far, over_right, over_left, far_a, far_b], parts)
    rows_full = jnp.stack([own_rows, down1, down2, down3, z_far, up3, up2, up1])
    reduced = scattered_along_z(parts)

    received = across_core(reduced)
    received = jnp.concatenate([received[:, edge:], received[:, :edge]], axis=1)
    halves = [dot(rows_full, half, ((1,), (1,))) for half in (reduced, received)]
    halves = [jnp.transpose(half, (0, 2, 1)) for half in halves]

    def ordered(value, other):
        return jnp.where(
            c == 0,
            jnp.concatenate([value, other], axis=0),
            jnp.concatenate([other, value], axis=0),
        )

    summed = scattered_in_plane(jnp.concatenate(halves, axis=1))
    cross_part = -ordered(reduced[:, :edge], received[:, :edge])
    inverse_part = diag_inverse[0] + ordered(summed[:TILE], summed[TILE:])
    return (cross_part[None], inverse_part[None])


def solution(mesh):
    return jax.shard_map(
        per_device,
        mesh=mesh,
        in_specs=(
            P("row", ("sec", "col")),
            P("sec", "row", "col"),
            P("sec", "col", "row"),
            P(),
            P(),
            P(),
        ),
        out_specs=(P("sec", "col", "row"), P("sec", "col", "row")),
        check_vma=False,
    )
```

```python
import functools

import jax
import jax.numpy as jnp
from jax import lax
from jax.experimental import pallas as pl
from jax.experimental.pallas import tpu as pltpu
from jax.sharding import PartitionSpec as P


TILE = 128
SLOTS = 4


Z, Y, X, CORES = 8, 2, 4, 2


def row_of(y, x, c):
    return (y % Y) * X * CORES + (x % X) * CORES + c


def row_pairs(move):
    places = [(y, x, c) for y in range(Y) for x in range(X) for c in range(CORES)]
    return [(row_of(*place), row_of(*move(*place))) for place in places]


def along_x(value, step):
    return lax.ppermute(value, "row", row_pairs(lambda y, x, c: (y, x + step, c)))


def across_y(value):
    return lax.ppermute(value, "row", row_pairs(lambda y, x, c: (y + 1, x, c)))


def across_core(value):
    return lax.ppermute(value, "row", row_pairs(lambda y, x, c: (y, x, 1 - c)))


def across_sec(value):
    return lax.ppermute(value, "sec", [(0, 1), (1, 0)])


def along_z(value, step):
    return lax.ppermute(value, "col", [(z, (z + step) % Z) for z in range(Z)])


def dot(left, right, dims):
    return lax.dot_general(
        left,
        right,
        (dims, ((), ())),
        precision=lax.Precision.HIGH,
        preferred_element_type=jnp.float32,
    )


def pick_kernel(place, ancestor, out, sems):
    tiles = [(a, b) for a in range(SLOTS) for b in range(SLOTS)]

    def spot(a, b):
        return (pl.ds(a * TILE, TILE), pl.ds(b * TILE, TILE))

    copies = []
    for a, b in tiles:
        first = pl.multiple_of(place[0, a] * TILE, TILE)
        second = pl.multiple_of(place[1, b] * TILE, TILE)
        source = ancestor.at[pl.ds(first, TILE), pl.ds(second, TILE)]
        copies.append(pltpu.make_async_copy(source, out.at[spot(a, b)], sems.at[a, b]))
        copies[-1].start()
    for (a, b), copy in zip(tiles, copies):
        copy.wait()
        out[spot(a, b)] = out[spot(a, b)] * place[2 + a, b].astype(jnp.float32)


def places(frontier, counts, pattern, block, group):
    ids = jnp.arange(SLOTS, dtype=jnp.int32)

    def at(table, index):
        return lax.dynamic_index_in_dim(table, index, 1, keepdims=False)

    row_live = ids[None, :] < at(counts, group)[:, None]
    column_live = ids[None, :] < at(counts, block)[:, None]
    start = (jnp.int32(0), group * SLOTS, block * SLOTS)
    near = lax.dynamic_slice(pattern, start, (2, SLOTS, SLOTS))
    mask = jnp.where(row_live[:, :, None] & column_live[:, None, :], near, 0)
    return jnp.concatenate([at(frontier, group)[:, None], at(frontier, block)[:, None], mask], axis=1)


def pick_tiles(ancestor, place):
    edge = SLOTS * TILE
    return pl.pallas_call(
        pick_kernel,
        grid_spec=pltpu.PrefetchScalarGridSpec(
            num_scalar_prefetch=1,
            grid=(),
            in_specs=[pl.BlockSpec(memory_space=pl.ANY)],
            out_specs=pl.BlockSpec(memory_space=pltpu.VMEM),
            scratch_shapes=[pltpu.SemaphoreType.DMA((SLOTS, SLOTS))],
        ),
        out_shape=jax.ShapeDtypeStruct((edge, edge), jnp.float32),
        cost_estimate=pl.CostEstimate(
            flops=edge * edge, bytes_accessed=8 * edge * edge, transcendentals=0
        ),
        compiler_params=pltpu.CompilerParams(vmem_limit_bytes=6 * 2**20),
        name="pick_tiles",
    )(place, ancestor)


def two_terms(value):
    high = value.astype(jnp.bfloat16)
    return high, (value - high.astype(jnp.float32)).astype(jnp.bfloat16)


def split_kernel(mine, partner, sibling_mine, sibling_partner, high, low):
    edge = SLOTS * TILE
    for i, row in enumerate(((mine, partner), (sibling_mine, sibling_partner))):
        for j, ref in enumerate(row):
            spot = (pl.ds(i * edge, edge), pl.ds(j * edge, edge))
            high[spot], low[spot] = two_terms(ref[...])


def split_tiles(*tiles):
    edge = SLOTS * TILE
    shape = jax.ShapeDtypeStruct((2 * edge, 2 * edge), jnp.bfloat16)
    return pl.pallas_call(
        split_kernel,
        out_shape=(shape, shape),
        cost_estimate=pl.CostEstimate(flops=12 * edge * edge, bytes_accessed=32 * edge * edge, transcendentals=0),
        compiler_params=pltpu.CompilerParams(vmem_limit_bytes=20 * 2**20),
        name="split_tiles",
    )(*tiles)


STEP = 512


def partial_kernel(spots, where, *refs):
    count = len(spots)
    blocks, (high, low) = refs[:count], refs[count : count + 2]
    parts, block_high, block_low, total, sems = refs[-5:]
    edge = SLOTS * TILE
    k = pl.program_id(0)
    y, x, z, c, flip = (where[i] for i in range(5))

    @pl.when(k == 0)
    def _():
        for j in range(count):
            for half in range(2):
                start = pl.multiple_of((half ^ flip) * edge, edge)
                value = blocks[j][pl.ds(start, edge), :]
                spot = (pl.ds(j * TILE, TILE), pl.ds(half * edge, edge))
                block_high[spot], block_low[spot] = two_terms(value.T)

    def product(left, right):
        return lax.dot_general(
            left[...], right[...], (((1,), (1,)), ((), ())), preferred_element_type=jnp.float32
        )

    total[k] = product(block_high, high) + product(block_low, high) + product(block_high, low)

    def copies(step):
        columns = pl.ds(pl.multiple_of(step * STEP, STEP), STEP)
        found = []
        for j, (dy, dx) in enumerate(spots):
            chip = lax.rem(y + dy, Y) * X + lax.rem(x + dx, X)
            distance = lax.rem(chip + 16 - 2 * z + 4 * c, Z)
            source = total.at[step, pl.ds(j * TILE, TILE), :]
            target = parts.at[distance, :, columns]
            found.append(pltpu.make_async_copy(source, target, sems.at[step, j]))
        return found

    for copy in copies(k):
        copy.start()

    @pl.when(k == pl.num_programs(0) - 1)
    def _():
        @pl.loop(0, 2 * edge // STEP)
        def _(step):
            for copy in copies(step):
                copy.wait()


def partial_products(spots, blocks, where, high, low, parts=None):
    count = len(spots)
    edge = SLOTS * TILE
    steps = 2 * edge // STEP
    vmem = pl.BlockSpec(memory_space=pltpu.VMEM)
    anywhere = pl.BlockSpec(memory_space=pl.ANY)
    tile_rows = pl.BlockSpec((STEP, 2 * edge), lambda k, where: (k, 0))
    args = [where, *blocks, high, low]
    if parts is not None:
        args.append(parts)
    rows = count * TILE
    return pl.pallas_call(
        functools.partial(partial_kernel, spots),
        grid_spec=pltpu.PrefetchScalarGridSpec(
            num_scalar_prefetch=1,
            grid=(steps,),
            in_specs=[vmem] * len(blocks) + [tile_rows] * 2 + [anywhere] * (parts is not None),
            out_specs=anywhere,
            scratch_shapes=[
                pltpu.VMEM((rows, 2 * edge), jnp.bfloat16),
                pltpu.VMEM((rows, 2 * edge), jnp.bfloat16),
                pltpu.VMEM((steps, rows, STEP), jnp.float32),
                pltpu.SemaphoreType.DMA((steps, count)),
            ],
        ),
        out_shape=jax.ShapeDtypeStruct((Z, TILE, 2 * edge), jnp.float32),
        input_output_aliases={} if parts is None else {len(args) - 1: 0},
        cost_estimate=pl.CostEstimate(
            flops=6 * rows * 4 * edge * edge,
            bytes_accessed=4 * edge * (4 * edge + 4 * rows),
            transcendentals=0,
        ),
        compiler_params=pltpu.CompilerParams(vmem_limit_bytes=24 * 2**20),
        name="partial_products",
    )(*args)


def to_chips(panel):
    low, high = panel[:, :TILE], panel[:, TILE:]
    y = lax.axis_index("row") // (X * CORES)
    first = jnp.where(y == 0, low, high)
    second = jnp.where(y == 0, high, low)

    def pairs(flip):
        found = []
        for z in range(Z):
            for g in range(16):
                c = (g // Z) ^ flip
                chip = (z + g % Z + 4 * c) % Z
                found.append((z * 16 + g, z * 16 + chip * CORES + c))
        return found

    first = lax.ppermute(first, ("col", "row"), pairs(0))
    second = lax.ppermute(second, ("col", "row"), pairs(1))
    return first, second


def mirrored(value):
    pairs = []
    for z in range(Z):
        for chip in range(8):
            for c in range(CORES):
                place = chip * CORES + c
                pairs.append((z * 16 + place, (chip - z + 4 * c) % Z * 16 + place))
    return lax.ppermute(value, ("col", "row"), pairs)


def scattered_along_z(parts):
    half = parts.shape[1] // 2

    def term(distance, which):
        return parts[distance % Z, which * half : (which + 1) * half]

    up_a, down_b = along_z(term(4, 0), 1), along_z(term(4, 1), -1)
    up_b, down_a = along_z(term(3, 1), 1), along_z(term(-3, 0), -1)
    for distance in (3, 2, 1):
        sums = up_a + term(distance, 0), down_b + term(-distance, 1)
        up_a, down_b = along_z(sums[0], 1), along_z(sums[1], -1)
        if distance > 1:
            up_b, down_a, *_ = together(up_b, down_a, *sums)
            sums = up_b + term(distance - 1, 1), down_a + term(1 - distance, 0)
            up_b, down_a = along_z(sums[0], 1), along_z(sums[1], -1)
            up_a, down_b, *_ = together(up_a, down_b, *sums)
    return jnp.concatenate([term(0, 0) + up_a + down_a, term(0, 1) + up_b + down_b], axis=0)


def scattered_in_plane(terms):
    groups = []
    for z in range(Z):
        for c in range(CORES):
            groups.append([z * 16 + (z + d) % Z * CORES + c for d in range(Z)])
    arrived = lax.all_to_all(terms, ("col", "row"), 0, 0, axis_index_groups=groups, tiled=True)
    return jnp.sum(arrived, axis=0)


def together(*values):
    return lax.optimization_barrier(values)


def per_device(ancestor, panel, diag_inverse, frontier, counts, pattern):
    s = lax.axis_index("sec")
    z = lax.axis_index("col")
    row = lax.axis_index("row")
    y, x, c = row // 8, row // 2 % 4, row % 2
    edge = SLOTS * TILE

    both_places = places(frontier, counts, pattern, s * Z + z, row)

    def pick(child):
        place = lax.dynamic_index_in_dim(both_places, child, 0, keepdims=False)
        return pick_tiles(ancestor, place)

    low, high = panel[0][:, :TILE], panel[0][:, TILE:]
    first, second = to_chips(panel[0])
    sibling_rows = across_core(jnp.where(c == 0, high, low))
    own_rows = jnp.concatenate([jnp.where(c == 0, low, high), sibling_rows], axis=0)
    up1 = along_z(own_rows, 1)
    down1 = along_z(own_rows, -1)
    theirs = pick(1 - s)
    partner = across_sec(theirs)
    own_columns = mirrored(jnp.concatenate([first, second], axis=0))
    mine = pick(s)
    sibling_mine = across_core(mine)
    sibling_partner = across_core(partner)
    tiles_high, tiles_low = split_tiles(mine, partner, sibling_mine, sibling_partner)

    where = jnp.stack([y, x, z, c, s ^ c]).astype(jnp.int32)

    def placed(spots, blocks, parts=None):
        return partial_products(spots, blocks, where, tiles_high, tiles_low, parts)

    left = along_x(own_columns, 1)
    right = along_x(own_columns, -1)
    over = across_y(own_columns)
    far = along_x(own_columns, 2)
    up2 = along_z(up1, 1)
    down2 = along_z(down1, -1)
    over_left = along_x(over, 1)
    over_right = along_x(over, -1)
    corner = across_y(far)
    up3 = along_z(up2, 1)
    down3 = along_z(down2, -1)
    parts = placed(((0, 3), (0, 1), (0, 2), (0, 0)), [left, right, far, own_columns])
    z_far = along_z(up3, 1)
    spots = ((1, 0), (1, 1), (1, 3), (1, 2))
    parts = placed(spots, [over, over_right, over_left, corner], parts)
    rows_full = jnp.stack([own_rows, down1, down2, down3, z_far, up3, up2, up1])
    reduced = scattered_along_z(parts)

    received = across_core(reduced)
    received = jnp.concatenate([received[:, edge:], received[:, :edge]], axis=1)
    halves = [dot(rows_full, half, ((1,), (1,))) for half in (reduced, received)]
    halves = [jnp.transpose(half, (0, 2, 1)) for half in halves]

    def ordered(value, other):
        return jnp.where(
            c == 0,
            jnp.concatenate([value, other], axis=0),
            jnp.concatenate([other, value], axis=0),
        )

    summed = scattered_in_plane(jnp.concatenate(halves, axis=1))
    cross_part = -ordered(reduced[:, :edge], received[:, :edge])
    inverse_part = diag_inverse[0] + ordered(summed[:TILE], summed[TILE:])
    return (cross_part[None], inverse_part[None])


def solution(mesh):
    return jax.shard_map(
        per_device,
        mesh=mesh,
        in_specs=(
            P("row", ("sec", "col")),
            P("sec", "row", "col"),
            P("sec", "col", "row"),
            P(),
            P(),
            P(),
        ),
        out_specs=(P("sec", "col", "row"), P("sec", "col", "row")),
        check_vma=False,
    )
```
